32 devices in a mesh: row: 4 (over x, core), col: 8 (over z, y).
Axes of the slice: x: 2, y: 2, z: 4, core: 2. Of those that a mesh axis runs over, the one named last changes fastest.
Arguments:
- design: bfloat16 [18432, 2048], P(('row', 'col')), may hold values from -0.19921875 to 0.19921875
- arc_filter: bfloat16 [2048, 2048], replicated, may hold values from -0.59765625 to 0.59765625
- arc_of_row: int32 [2048], replicated, may hold values from 0 to 255, never falling along the last dimension, each value on 1 to 512 neighbouring positions
- terr_stored: bfloat16 [18432, 128], P(('row', 'col')), may hold values from -3 to 3
- block_order: int32 [144], P('row'), may hold values from 0 to 143, as said below
- directions: float32 [18432, 256], P(('row', 'col')), may hold values from -6 to 6
Outputs:
- normals: float32 [4, 8, 576, 18432], P(None, 'col', None, 'row')
- products: float32 [18432, 256], P(('row', 'col'))
The draws below stay inside these ranges and needn't reach their ends.
Inputs may be any that keep to these rules, and one draw needn't show every extreme that they name: `arc_of_row`: arc numbers never fall along the observations. `block_order`: each aligned group of 36 consecutive entries (the blocks of one block of 4608 unknowns) is a permutation of the positions of that same group.
All inputs are finite; a program needn't handle non-finite values.
Results may differ from the reference program's by a relative error of at most 0.00045.
Values may be sent and summed in bfloat16 or wider, within the bound.
A program may use at most 192 MiB of HBM per device.

```python
import math
import jax
import jax.numpy as jnp
import numpy as np
from jax import lax

M = 18432
BLK = 128
K = 2048
P_SIZE = 256
NQ = 144
QR = 36
N_ROW = 4
N_COL = 8


def draw_block_order(key, part):
    group_keys = jax.random.split(jax.random.fold_in(key, 17), NQ // QR)
    permuted = jax.vmap(lambda single: jax.random.permutation(single, QR))(group_keys)
    offsets = jnp.arange(NQ // QR, dtype=jnp.int32)[:, None] * QR
    return (permuted.astype(jnp.int32) + offsets).reshape(NQ).astype(jnp.int32)


def levels(rng, shape, shards, low, top_value):
    factor_of = 1.0
    for position, parts in shards:
        steps = jax.random.uniform(jax.random.fold_in(jax.random.fold_in(rng, 6), position), (parts,), jnp.float32, low / len(shards), top_value / len(shards))
        factor_of = factor_of * jnp.repeat(jnp.exp(steps), shape[position] // parts).reshape((-1,) + (1,) * (len(shape) - 1 - position))
    return factor_of


def split_up(number_of, total, limit, lean):
    weights = [(1 << 20) // math.isqrt(standing ** lean) + 1 for standing in range(2, number_of + 1)]
    rest, given = total - limit - (number_of - 1), [1] * (number_of - 1)
    while rest > 0:
        free = [i for i in range(number_of - 1) if given[i] < limit]
        mass, remaining = sum([weights[i] for i in free]), rest
        for i in free:
            addition = min(limit - given[i], max(1, remaining * weights[i] // mass), rest)
            given[i] = given[i] + addition
            rest = rest - addition
    return np.array([limit] + given)


def ragged_sizes(stream_key, amount, total, reach, skew):
    if amount == 2:
        one = jax.random.randint(stream_key, (), max(1, total - reach), min(reach, total - 1) + 1)
        return jnp.stack([one, total - one])
    sizes = jnp.asarray(split_up(amount, total, reach, skew), jnp.int32)
    pairs = (amount - 1) // 2
    source_of, sink = sizes[1:1 + 2 * pairs:2], sizes[2:2 + 2 * pairs:2]
    margin = jnp.minimum(source_of - 1, reach - sink)
    moved = jax.random.randint(jax.random.fold_in(stream_key, 1), (pairs,), 0, 1 << 20) % (margin + 1)
    sizes = sizes.at[1:1 + 2 * pairs:2].set(source_of - moved).at[2:2 + 2 * pairs:2].set(sink + moved)
    return sizes[jax.random.permutation(jax.random.fold_in(stream_key, 2), amount)]


def scatter_about(key, extent, scale, reach, shards=(), held_as=jnp.bfloat16):
    drawn = jax.random.normal(key, extent, jnp.float32) * scale
    if len(shards) > 0:
        drawn = levels(key, extent, shards, -0.22, 0.18) * drawn
    return jnp.clip(drawn, min=-reach, max=reach).astype(held_as)


def setup_inputs(seed: int = 0) -> dict:
    keys = jax.random.split(jax.random.key(seed), 7)
    design = scatter_about(keys[0], (M, K), 0.03125, 0.19921875, ((0, 32),))
    arc_filter = scatter_about(keys[1], (K, K), 0.1, 0.59765625)
    arc_of_row = jnp.searchsorted(jnp.cumsum(ragged_sizes(keys[2], K // 8, K, K // 4, 2)), jnp.arange(K), side="right").astype(jnp.int32)
    terr_stored = scatter_about(keys[3], (M, BLK), 0.5, 3.0, ((0, 32),))
    block_order = draw_block_order(jax.random.fold_in(keys[6], 71), 0)
    directions = scatter_about(keys[5], (M, P_SIZE), 1.0, 6.0, ((0, 32),), jnp.float32)
    return {"design": design, "arc_filter": arc_filter, "arc_of_row": arc_of_row, "terr_stored": terr_stored, "block_order": block_order, "directions": directions}


def whiten(design, arc_filter, arc_of_row):
    positions = jnp.arange(arc_filter.shape[0], dtype=jnp.int32)
    keep_mask = (positions[:, None] > positions[None, :]) & (arc_of_row[:, None] == arc_of_row[None, :])
    lower_part = jnp.where(keep_mask, arc_filter, jnp.zeros_like(arc_filter))
    mixed_part = lax.dot_general(design, lower_part, (((1,), (1,)), ((), ())), preferred_element_type=jnp.float32)
    return (design.astype(jnp.float32) + mixed_part).astype(jnp.bfloat16)


def reference(design, arc_filter, arc_of_row, terr_stored, block_order, directions):
    whitened = whiten(design, arc_filter, arc_of_row)
    gram = lax.dot_general(whitened, whitened, (((1,), (1,)), ((), ())), preferred_element_type=jnp.float32)
    stored = terr_stored.astype(jnp.float32).reshape(NQ, BLK, BLK)
    symmetric = jnp.triu(stored) + jnp.swapaxes(jnp.triu(stored, 1), 1, 2)
    ordered = jnp.zeros_like(symmetric).at[block_order].set(symmetric)
    blocked = gram.reshape(NQ, BLK, NQ, BLK)
    diagonal_index = jnp.arange(NQ, dtype=jnp.int32)
    blocked = blocked.at[diagonal_index, :, diagonal_index, :].add(ordered)
    normal_full = blocked.reshape(M, M)
    products = jnp.dot(normal_full, directions, precision=lax.Precision.HIGHEST, preferred_element_type=jnp.float32)
    return normal_full.reshape(N_ROW, N_COL, M // (N_ROW * N_COL), M), products
```

```python
import functools

import jax
import jax.numpy as jnp
import numpy as np
from jax import lax
from jax.experimental import pallas as pl
from jax.experimental.pallas import tpu as pltpu
from jax.sharding import PartitionSpec as P


HIGH = lax.Precision.HIGHEST
NT = (((1,), (1,)), ((), ()))


def dot_high(a, b):
    return jnp.dot(a, b, precision=HIGH, preferred_element_type=jnp.float32)


def whiten(design, arc_filter, arc_of_row):
    positions = jnp.arange(arc_filter.shape[0], dtype=jnp.int32)
    keep_mask = (positions[:, None] > positions[None, :]) & (
        arc_of_row[:, None] == arc_of_row[None, :]
    )
    lower_part = jnp.where(keep_mask, arc_filter, jnp.zeros_like(arc_filter))
    mixed_part = lax.dot_general(design, lower_part, NT, preferred_element_type=jnp.float32)
    return (design.astype(jnp.float32) + mixed_part).astype(jnp.bfloat16)


def general_body(design, arc_filter, arc_of_row, terr_stored, block_order, directions):
    whitened = whiten(design, arc_filter, arc_of_row)
    own_width = whitened.shape[0]
    rows_block, terr_rows = (
        lax.all_gather(whitened, "col", axis=0, tiled=True),
        lax.all_gather(terr_stored, "col", axis=0, tiled=True),
    )
    cols_block = lax.all_gather(whitened, "row", axis=0, tiled=True)
    normal_tile = lax.dot_general(cols_block, rows_block, NT, preferred_element_type=jnp.float32)
    block_size = terr_rows.shape[1]
    span_rows = terr_rows.shape[0]
    group_count = span_rows // block_size
    row_index = lax.axis_index("row")
    col_index = lax.axis_index("col")
    local_order = block_order - row_index * group_count
    selector = (local_order[None, :] == jnp.arange(group_count, dtype=jnp.int32)[:, None]).astype(
        jnp.float32
    )
    stored = terr_rows.astype(jnp.float32).reshape(group_count, block_size, block_size)
    symmetric = jnp.triu(stored) + jnp.swapaxes(jnp.triu(stored, 1), 1, 2)
    ordered = jnp.einsum("qt,tab->qab", selector, symmetric, precision=HIGH).reshape(
        span_rows, block_size
    )
    own_rows = lax.dynamic_slice_in_dim(ordered, col_index * own_width, own_width, 0)
    positions = col_index * own_width + jnp.arange(own_width, dtype=jnp.int32)
    onehot = (
        (positions // block_size)[:, None] == jnp.arange(group_count, dtype=jnp.int32)[None, :]
    ).astype(jnp.float32)
    terr_added = (onehot[:, :, None] * own_rows[:, None, :]).reshape(own_width, span_rows)
    current = lax.dynamic_slice_in_dim(normal_tile, row_index * own_width, own_width, 0)
    normal_tile = lax.dynamic_update_slice_in_dim(
        normal_tile, current + terr_added, row_index * own_width, 0
    )
    tile_rows = normal_tile.shape[0]
    partial_sum = dot_high(normal_tile, lax.all_gather(directions, "col", axis=0, tiled=True))
    products = lax.psum_scatter(partial_sum, "row", scatter_dimension=0, tiled=True)
    normals = normal_tile.reshape(tile_rows // own_width, 1, own_width, span_rows)
    return (normals, products)


def whiten_kernel(d_ref, dp_ref, f_ref, fp_ref, ac_ref, ar_ref, arp_ref, top_ref, low_ref):
    b = pl.program_id(0)
    width = f_ref.shape[0]
    half = top_ref.shape[0]
    zero = jnp.zeros((width, width), jnp.float32)
    k = lax.broadcasted_iota(jnp.int32, (width, width), 0)
    j = lax.broadcasted_iota(jnp.int32, (width, width), 1)
    keep = (k > j) & (ac_ref[...] == ar_ref[...])
    keep_prev = (ac_ref[...] == arp_ref[...]) & (b > 0)
    here = jnp.where(keep, f_ref[...].astype(jnp.float32), zero).astype(jnp.bfloat16)
    prev = jnp.where(keep_prev, fp_ref[...].astype(jnp.float32), zero).astype(jnp.bfloat16)
    mixed = lax.dot_general(d_ref[...], here, NT, preferred_element_type=jnp.float32)
    mixed += lax.dot_general(dp_ref[...], prev, NT, preferred_element_type=jnp.float32)
    out = (d_ref[...].astype(jnp.float32) + mixed).astype(jnp.bfloat16)
    top_ref[...] = out[:half]
    low_ref[...] = out[half:]


def whiten_halves(design, arc_filter, arc_of_row):
    own, total = design.shape
    width = total // 4
    half = own // 2
    here = lambda b: (0, b)
    prev = lambda b: (0, jnp.maximum(b - 1, 0))
    out = jax.ShapeDtypeStruct((half, total), jnp.bfloat16)
    row = arc_of_row.reshape(1, total)
    return pl.pallas_call(
        whiten_kernel,
        grid=(total // width,),
        in_specs=[
            pl.BlockSpec((own, width), here),
            pl.BlockSpec((own, width), prev),
            pl.BlockSpec((width, width), lambda b: (b, b)),
            pl.BlockSpec((width, width), lambda b: (b, jnp.maximum(b - 1, 0))),
            pl.BlockSpec((width, 1), lambda b: (b, 0)),
            pl.BlockSpec((1, width), here),
            pl.BlockSpec((1, width), prev),
        ],
        out_specs=[pl.BlockSpec((half, width), here)] * 2,
        out_shape=[out, out],
        name="whiten",
        cost_estimate=pl.CostEstimate(
            flops=4 * own * total * width, bytes_accessed=8 * own * total, transcendentals=0
        ),
    )(design, design, arc_filter, arc_filter, arc_of_row.reshape(total, 1), row, row)


def tile_kernel(cands, first, tile, s_ref, *refs):
    n = len(cands)
    bufs = refs[: 2 * n]
    a_ref, t_ref = refs[2 * n : 2 * n + 2]
    rest = refs[2 * n + 2 :]
    o_ref, b_ref, sem = rest if first else rest[1:]
    i = pl.program_id(0)
    half = bufs[0].shape[0]

    def copy(src, y, h):
        spot = (2 * y + h) * half
        return pltpu.make_async_copy(src, b_ref.at[pl.ds(spot, half)], sem.at[2 * y + h])

    @pl.when(i == 0)
    def _():
        for y in range(2):
            for q, cand in enumerate(cands):

                @pl.when(s_ref[1 + y] == cand)
                def _():
                    copy(bufs[2 * q], y, 0).start()
                    copy(bufs[2 * q + 1], y, 1).start()

        for y in range(2):
            for h in range(2):
                copy(bufs[h], y, h).wait()

    @pl.loop(0, o_ref.shape[1] // tile)
    def _(t):
        span = pl.ds(pl.multiple_of(t * tile, tile), tile)
        o_ref[:, span] = lax.dot_general(
            a_ref[0], b_ref[span, :], NT, preferred_element_type=jnp.float32
        )

    @pl.when((i == 0) & (s_ref[3] == 1))
    def _():
        o_ref[...] += t_ref[...]


def tile_job(scalars, cands, bufs, rows, terr, out):
    count, own, total = rows.shape
    span = 2 * own
    tile = next(t for t in (384, 256, 128) if span % t == 0)
    first = not isinstance(out, jax.Array)
    any_spec = pl.BlockSpec(memory_space=pl.ANY)
    operands = [b for c in cands for b in bufs[c]]
    in_specs = [any_spec] * len(operands) + [
        pl.BlockSpec((1, own, total), lambda i, s: (i, 0, 0)),
        pl.BlockSpec((own, span), lambda i, s: (0, 0)),
    ]
    operands += [rows, terr]
    shape = out
    alias = {}
    if not first:
        alias = {1 + len(operands): 0}
        operands.append(out)
        in_specs.append(any_spec)
        shape = jax.ShapeDtypeStruct(out.shape, out.dtype)
    return pl.pallas_call(
        functools.partial(tile_kernel, cands, first, tile),
        grid_spec=pltpu.PrefetchScalarGridSpec(
            num_scalar_prefetch=1,
            grid=(count,),
            in_specs=in_specs,
            out_specs=pl.BlockSpec((own, span), lambda i, s: (s[4 + i], s[0])),
            scratch_shapes=[
                pltpu.VMEM((span, total), jnp.bfloat16),
                pltpu.SemaphoreType.DMA((4,)),
            ],
        ),
        out_shape=shape,
        input_output_aliases=alias,
        name="gram_tile",
        compiler_params=pltpu.CompilerParams(vmem_limit_bytes=48 * 1024 * 1024),
        cost_estimate=pl.CostEstimate(
            flops=2 * count * own * span * total,
            bytes_accessed=2 * count * own * total + 4 * count * own * span,
            transcendentals=0,
        ),
    )(scalars, *operands)


def ring_body(n_row, n_col, design, arc_filter, arc_of_row, terr_stored, block_order, directions):
    own, total = design.shape
    block = terr_stored.shape[1]
    r = lax.axis_index("row")
    c = lax.axis_index("col")
    z, y = c // 2, c % 2
    zs = n_col // 2
    half = own // 2

    def swap(a, axis, mask):
        n = n_row if axis == "row" else n_col
        return lax.ppermute(a, axis, [(i, i ^ mask) for i in range(n)])

    col_of = [2 * p if p < zs else 2 * (n_col - 1 - p) + 1 for p in range(n_col)]
    forward = [(col_of[p], col_of[(p + 1) % n_col]) for p in range(n_col)]
    backward = [(d, s) for s, d in forward]
    far = n_col // 2

    top, low = whiten_halves(design, arc_filter, arc_of_row)
    bufs = {0: (top, low)}
    up = down = (top, low)
    for k in range(1, far):
        up = tuple(lax.ppermute(h, "col", forward) for h in up)
        down = tuple(lax.ppermute(h, "col", backward) for h in down)
        bufs[n_col - k], bufs[k] = up, down
    bufs[far] = (lax.ppermute(up[0], "col", forward), lax.ppermute(down[1], "col", backward))

    across = {0: (top, low)}
    mask = n_row // 2
    while mask:
        for m in list(across):
            across[m | mask] = tuple(swap(h, "row", mask) for h in across[m])
        mask //= 2
    rows = jnp.concatenate([h for m in range(n_row) for h in across[m]], 0)
    rows = rows.reshape(n_row, own, total)

    other = swap(terr_stored, "col", 1)
    terr_pair = jnp.where(
        y == 0,
        jnp.concatenate([terr_stored, other], 0),
        jnp.concatenate([other, terr_stored], 0),
    )
    pairs = terr_pair[None]
    mask = 1
    while mask < zs:
        pairs = jnp.concatenate([pairs, swap(pairs, "col", 2 * mask)], 0)
        mask *= 2
    per_pair = 2 * own // block
    count = per_pair * zs
    local_order = (block_order - r * count).reshape(zs, per_pair)[
        jnp.bitwise_xor(z, jnp.arange(zs, dtype=jnp.int32))
    ].reshape(count)
    wanted = z * per_pair + jnp.arange(per_pair, dtype=jnp.int32)
    selector = (local_order[None, :] == wanted[:, None]).astype(jnp.bfloat16)
    picked = jnp.einsum(
        "qt,tab->qab",
        selector,
        pairs.reshape(count, block, block),
        preferred_element_type=jnp.float32,
    )
    symmetric = (jnp.triu(picked) + jnp.swapaxes(jnp.triu(picked, 1), 1, 2)).reshape(2 * own, block)
    own_rows = lax.dynamic_slice_in_dim(symmetric, y * own, own, 0)
    positions = y * own + jnp.arange(own, dtype=jnp.int32)
    onehot = (
        (positions // block)[:, None] == jnp.arange(per_pair, dtype=jnp.int32)[None, :]
    ).astype(jnp.float32)
    terr = (onehot[:, :, None] * own_rows[:, None, :]).reshape(own, 2 * own)

    v = lax.dot_general(
        jnp.concatenate([top, low], 0).astype(jnp.float32),
        directions,
        (((0,), (0,)), ((), ())),
        precision=HIGH,
        preferred_element_type=jnp.float32,
    )
    mask = 1
    masks = []
    while mask < n_row:
        masks.append(mask)
        bit = (r // mask) % 2
        part = v.shape[0] // 2
        given = lax.dynamic_slice_in_dim(v, (1 - bit) * part, part, 0)
        v = lax.dynamic_slice_in_dim(v, bit * part, part, 0) + swap(given, "row", mask)
        mask *= 2
    part = v.shape[0] // n_col
    piece = lax.dynamic_slice_in_dim(v, c * part, part, 0)
    for m in range(1, n_col):
        given = lax.dynamic_slice_in_dim(v, jnp.bitwise_xor(c, m) * part, part, 0)
        piece = piece + swap(given, "col", m)
    v = jnp.zeros_like(v)
    for m in range(n_col):
        got = piece if m == 0 else swap(piece, "col", m)
        v = lax.dynamic_update_slice_in_dim(v, got, jnp.bitwise_xor(c, m) * part, 0)
    for mask in reversed(masks):
        got = swap(v, "row", mask)
        bit = (r // mask) % 2
        v = jnp.where(bit == 0, jnp.concatenate([v, got], 0), jnp.concatenate([got, v], 0))
    edge = min(block, own)
    got = swap(jnp.where(y == 0, directions[own - edge :], directions[:edge]), "col", 1)
    gap = jnp.zeros((own - edge, directions.shape[1]), directions.dtype)
    near = jnp.where(
        y == 0,
        jnp.concatenate([directions, got, gap], 0),
        jnp.concatenate([gap, got, directions], 0),
    )
    products = dot_high(jnp.concatenate([top, low], 0).astype(jnp.float32), v)
    products = products + dot_high(terr, near)

    pos_of = [0] * n_col
    for p, col in enumerate(col_of):
        pos_of[col] = p
    table = np.zeros((zs, n_col, 4), np.int32)
    for col in range(n_col):
        jobs = []
        for zz in range(zs):
            ks = [(pos_of[2 * zz + yy] - pos_of[col]) % n_col for yy in range(2)]
            ready = max(min(k, n_col - k) for k in ks)
            jobs.append((ready, zz, ks))
        for j, (_, zz, ks) in enumerate(sorted(jobs)):
            table[j, col] = [zz, ks[0], ks[1], int(zz == col // 2)]
    row_spots = jnp.bitwise_xor(r, jnp.arange(n_row, dtype=jnp.int32))
    out = jax.ShapeDtypeStruct((n_row * own, n_col * own), jnp.float32)
    for j in range(zs):
        cands = tuple(sorted(set(table[j, :, 1:3].ravel().tolist())))
        scalars = jnp.concatenate([jnp.asarray(table[j])[c], row_spots])
        out = tile_job(scalars, cands, bufs, rows, terr, out)
    return out.reshape(n_row, 1, own, n_col * own), products


def power_of_two(n):
    return n > 1 and n & (n - 1) == 0


def solution(mesh):
    n_row, n_col = mesh.shape["row"], mesh.shape["col"]

    def body(design, arc_filter, arc_of_row, terr_stored, block_order, directions):
        args = (design, arc_filter, arc_of_row, terr_stored, block_order, directions)
        own, block = design.shape[0], terr_stored.shape[1]
        aligned = own % 32 == 0 and (2 * own) % block == 0 and (2 * own) % 128 == 0
        if power_of_two(n_row) and power_of_two(n_col) and n_col > 2 and aligned:
            return ring_body(n_row, n_col, *args)
        return general_body(*args)

    return jax.shard_map(
        body,
        mesh=mesh,
        in_specs=(
            P(("row", "col"), None),
            P(),
            P(),
            P(("row", "col"), None),
            P("row"),
            P(("row", "col"), None),
        ),
        out_specs=(P(None, "col", None, "row"), P(("row", "col"), None)),
        check_vma=False,
    )
```

```python
import functools

import jax
import jax.numpy as jnp
import numpy as np
from jax import lax
from jax.experimental import pallas as pl
from jax.experimental.pallas import tpu as pltpu
from jax.sharding import PartitionSpec as P


HIGH = lax.Precision.HIGHEST
NT = (((1,), (1,)), ((), ()))


def dot_high(a, b):
    return jnp.dot(a, b, precision=HIGH, preferred_element_type=jnp.float32)


def whiten(design, arc_filter, arc_of_row):
    positions = jnp.arange(arc_filter.shape[0], dtype=jnp.int32)
    keep_mask = (positions[:, None] > positions[None, :]) & (
        arc_of_row[:, None] == arc_of_row[None, :]
    )
    lower_part = jnp.where(keep_mask, arc_filter, jnp.zeros_like(arc_filter))
    mixed_part = lax.dot_general(design, lower_part, NT, preferred_element_type=jnp.float32)
    return (design.astype(jnp.float32) + mixed_part).astype(jnp.bfloat16)


def general_body(design, arc_filter, arc_of_row, terr_stored, block_order, directions):
    whitened = whiten(design, arc_filter, arc_of_row)
    own_width = whitened.shape[0]
    rows_block, terr_rows = (
        lax.all_gather(whitened, "col", axis=0, tiled=True),
        lax.all_gather(terr_stored, "col", axis=0, tiled=True),
    )
    cols_block = lax.all_gather(whitened, "row", axis=0, tiled=True)
    normal_tile = lax.dot_general(cols_block, rows_block, NT, preferred_element_type=jnp.float32)
    block_size = terr_rows.shape[1]
    span_rows = terr_rows.shape[0]
    group_count = span_rows // block_size
    row_index = lax.axis_index("row")
    col_index = lax.axis_index("col")
    local_order = block_order - row_index * group_count
    selector = (local_order[None, :] == jnp.arange(group_count, dtype=jnp.int32)[:, None]).astype(
        jnp.float32
    )
    stored = terr_rows.astype(jnp.float32).reshape(group_count, block_size, block_size)
    symmetric = jnp.triu(stored) + jnp.swapaxes(jnp.triu(stored, 1), 1, 2)
    ordered = jnp.einsum("qt,tab->qab", selector, symmetric, precision=HIGH).reshape(
        span_rows, block_size
    )
    own_rows = lax.dynamic_slice_in_dim(ordered, col_index * own_width, own_width, 0)
    positions = col_index * own_width + jnp.arange(own_width, dtype=jnp.int32)
    onehot = (
        (positions // block_size)[:, None] == jnp.arange(group_count, dtype=jnp.int32)[None, :]
    ).astype(jnp.float32)
    terr_added = (onehot[:, :, None] * own_rows[:, None, :]).reshape(own_width, span_rows)
    current = lax.dynamic_slice_in_dim(normal_tile, row_index * own_width, own_width, 0)
    normal_tile = lax.dynamic_update_slice_in_dim(
        normal_tile, current + terr_added, row_index * own_width, 0
    )
    tile_rows = normal_tile.shape[0]
    partial_sum = dot_high(normal_tile, lax.all_gather(directions, "col", axis=0, tiled=True))
    products = lax.psum_scatter(partial_sum, "row", scatter_dimension=0, tiled=True)
    normals = normal_tile.reshape(tile_rows // own_width, 1, own_width, span_rows)
    return (normals, products)


def whiten_kernel(d_ref, dp_ref, f_ref, fp_ref, ac_ref, ar_ref, arp_ref, top_ref, low_ref):
    b = pl.program_id(0)
    width = f_ref.shape[0]
    half = top_ref.shape[0]
    zero = jnp.zeros((width, width), jnp.float32)
    k = lax.broadcasted_iota(jnp.int32, (width, width), 0)
    j = lax.broadcasted_iota(jnp.int32, (width, width), 1)
    keep = (k > j) & (ac_ref[...] == ar_ref[...])
    keep_prev = (ac_ref[...] == arp_ref[...]) & (b > 0)
    here = jnp.where(keep, f_ref[...].astype(jnp.float32), zero).astype(jnp.bfloat16)
    prev = jnp.where(keep_prev, fp_ref[...].astype(jnp.float32), zero).astype(jnp.bfloat16)
    mixed = lax.dot_general(d_ref[...], here, NT, preferred_element_type=jnp.float32)
    mixed += lax.dot_general(dp_ref[...], prev, NT, preferred_element_type=jnp.float32)
    out = (d_ref[...].astype(jnp.float32) + mixed).astype(jnp.bfloat16)
    top_ref[...] = out[:half]
    low_ref[...] = out[half:]


def whiten_halves(design, arc_filter, arc_of_row):
    own, total = design.shape
    width = total // 4
    half = own // 2
    here = lambda b: (0, b)
    prev = lambda b: (0, jnp.maximum(b - 1, 0))
    out = jax.ShapeDtypeStruct((half, total), jnp.bfloat16)
    row = arc_of_row.reshape(1, total)
    return pl.pallas_call(
        whiten_kernel,
        grid=(total // width,),
        in_specs=[
            pl.BlockSpec((own, width), here),
            pl.BlockSpec((own, width), prev),
            pl.BlockSpec((width, width), lambda b: (b, b)),
            pl.BlockSpec((width, width), lambda b: (b, jnp.maximum(b - 1, 0))),
            pl.BlockSpec((width, 1), lambda b: (b, 0)),
            pl.BlockSpec((1, width), here),
            pl.BlockSpec((1, width), prev),
        ],
        out_specs=[pl.BlockSpec((half, width), here)] * 2,
        out_shape=[out, out],
        name="whiten",
        cost_estimate=pl.CostEstimate(
            flops=4 * own * total * width, bytes_accessed=8 * own * total, transcendentals=0
        ),
    )(design, design, arc_filter, arc_filter, arc_of_row.reshape(total, 1), row, row)


def tile_kernel(cands, first, tile, s_ref, *refs):
    n = len(cands)
    bufs = refs[: 2 * n]
    a_ref, t_ref = refs[2 * n : 2 * n + 2]
    rest = refs[2 * n + 2 :]
    o_ref, b_ref, sem = rest if first else rest[1:]
    i = pl.program_id(0)
    half = bufs[0].shape[0]

    def copy(src, y, h):
        spot = (2 * y + h) * half
        return pltpu.make_async_copy(src, b_ref.at[pl.ds(spot, half)], sem.at[2 * y + h])

    @pl.when(i == 0)
    def _():
        for y in range(2):
            for q, cand in enumerate(cands):

                @pl.when(s_ref[1 + y] == cand)
                def _():
                    copy(bufs[2 * q], y, 0).start()
                    copy(bufs[2 * q + 1], y, 1).start()

        for y in range(2):
            for h in range(2):
                copy(bufs[h], y, h).wait()

    @pl.loop(0, o_ref.shape[1] // tile)
    def _(t):
        span = pl.ds(pl.multiple_of(t * tile, tile), tile)
        o_ref[:, span] = lax.dot_general(
            a_ref[0], b_ref[span, :], NT, preferred_element_type=jnp.float32
        )

    @pl.when((i == 0) & (s_ref[3] == 1))
    def _():
        o_ref[...] += t_ref[...]


def tile_job(scalars, cands, bufs, rows, terr, out):
    count, own, total = rows.shape
    span = 2 * own
    tile = span
    first = not isinstance(out, jax.Array)
    any_spec = pl.BlockSpec(memory_space=pl.ANY)
    operands = [b for c in cands for b in bufs[c]]
    in_specs = [any_spec] * len(operands) + [
        pl.BlockSpec((1, own, total), lambda i, s: (i, 0, 0)),
        pl.BlockSpec((own, span), lambda i, s: (0, 0)),
    ]
    operands += [rows, terr]
    shape = out
    alias = {}
    if not first:
        alias = {1 + len(operands): 0}
        operands.append(out)
        in_specs.append(any_spec)
        shape = jax.ShapeDtypeStruct(out.shape, out.dtype)
    return pl.pallas_call(
        functools.partial(tile_kernel, cands, first, tile),
        grid_spec=pltpu.PrefetchScalarGridSpec(
            num_scalar_prefetch=1,
            grid=(count,),
            in_specs=in_specs,
            out_specs=pl.BlockSpec((own, span), lambda i, s: (s[4 + i], s[0])),
            scratch_shapes=[
                pltpu.VMEM((span, total), jnp.bfloat16),
                pltpu.SemaphoreType.DMA((4,)),
            ],
        ),
        out_shape=shape,
        input_output_aliases=alias,
        name="gram_tile",
        compiler_params=pltpu.CompilerParams(vmem_limit_bytes=48 * 1024 * 1024),
        cost_estimate=pl.CostEstimate(
            flops=2 * count * own * span * total,
            bytes_accessed=2 * count * own * total + 4 * count * own * span,
            transcendentals=0,
        ),
    )(scalars, *operands)


def ring_body(n_row, n_col, design, arc_filter, arc_of_row, terr_stored, block_order, directions):
    own, total = design.shape
    block = terr_stored.shape[1]
    r = lax.axis_index("row")
    c = lax.axis_index("col")
    z, y = c // 2, c % 2
    zs = n_col // 2

    def swap(a, axis, mask):
        n = n_row if axis == "row" else n_col
        return lax.ppermute(a, axis, [(i, i ^ mask) for i in range(n)])

    col_of = [2 * p if p < zs else 2 * (n_col - 1 - p) + 1 for p in range(n_col)]
    pos_of = [0] * n_col
    for p, col in enumerate(col_of):
        pos_of[col] = p
    forward = [(col_of[p], col_of[(p + 1) % n_col]) for p in range(n_col)]
    backward = [(d, s) for s, d in forward]
    far = n_col // 2

    terr_bufs = {0: terr_stored}

    def terr_step(k):
        up = terr_bufs[(n_col - k + 1) % n_col]
        terr_bufs[n_col - k] = lax.ppermute(up, "col", forward)
        if k < far:
            terr_bufs[k] = lax.ppermute(terr_bufs[k - 1], "col", backward)

    edge = min(block, own)
    got = swap(jnp.where(y == 0, directions[own - edge :], directions[:edge]), "col", 1)
    gap = jnp.zeros((own - edge, directions.shape[1]), directions.dtype)
    near = jnp.where(
        y == 0,
        jnp.concatenate([directions, got, gap], 0),
        jnp.concatenate([gap, got, directions], 0),
    )
    terr_step(1)
    terr_step(2)

    top, low = whiten_halves(design, arc_filter, arc_of_row)
    bufs = {0: [top, low]}
    for k in range(1, n_col):
        bufs[k] = [None, None]

    def ring_step(k, h):
        if k < far or h == 0:
            up = bufs[(n_col - k + 1) % n_col][h]
            bufs[n_col - k][h] = lax.ppermute(up, "col", forward)
        if k < far or h == 1:
            bufs[k][h] = lax.ppermute(bufs[k - 1][h], "col", backward)

    ring_step(1, 0)
    v = lax.dot_general(
        jnp.concatenate([top, low], 0).astype(jnp.float32),
        directions,
        (((0,), (0,)), ((), ())),
        precision=HIGH,
        preferred_element_type=jnp.float32,
    )
    masks = []
    mask = 1
    while mask < n_row:
        masks.append(mask)
        bit = (r // mask) % 2
        part = v.shape[0] // 2
        given = lax.dynamic_slice_in_dim(v, (1 - bit) * part, part, 0)
        v = lax.dynamic_slice_in_dim(v, bit * part, part, 0) + swap(given, "row", mask)
        mask *= 2
    part = v.shape[0] // n_col
    pieces = v.reshape(n_col, part, v.shape[1])[jnp.bitwise_xor(c, jnp.arange(n_col))]
    piece = pieces[0]
    for m in range(1, n_col):
        piece = piece + swap(pieces[m], "col", m)
    ring_step(1, 1)
    across = {0: (top, low)}
    mask = n_row // 2
    while mask:
        for m in list(across):
            across[m | mask] = tuple(swap(a, "row", mask) for a in across[m])
        mask //= 2
        if mask == n_row // 4:
            for k in range(3, far + 1):
                terr_step(k)
            got = [piece] + [swap(piece, "col", m) for m in range(1, n_col)]
            ring_step(2, 0)
            ring_step(2, 1)
    rows = jnp.concatenate([h for m in range(n_row) for h in across[m]], 0)
    rows = rows.reshape(n_row, own, total)
    v = jnp.stack(got)[jnp.bitwise_xor(c, jnp.arange(n_col))].reshape(-1, v.shape[1])
    for mask in reversed(masks):
        got = swap(v, "row", mask)
        bit = (r // mask) % 2
        v = jnp.where(bit == 0, jnp.concatenate([v, got], 0), jnp.concatenate([got, v], 0))
    for k in range(3, far + 1):
        ring_step(k, 0)
        ring_step(k, 1)

    per_pair = 2 * own // block
    count = per_pair * zs
    spots = np.array([[(pos_of[d] - pos_of[s]) % n_col for d in range(n_col)] for s in range(n_col)])
    stored = jnp.stack([terr_bufs[k] for k in range(n_col)])[jnp.asarray(spots, jnp.int32)[c]]
    local_order = block_order - r * count
    wanted = z * per_pair + jnp.arange(per_pair, dtype=jnp.int32)
    selector = (local_order[None, :] == wanted[:, None]).astype(jnp.bfloat16)
    picked = jnp.einsum(
        "qt,tab->qab",
        selector,
        stored.reshape(count, block, block),
        preferred_element_type=jnp.float32,
    )
    symmetric = (jnp.triu(picked) + jnp.swapaxes(jnp.triu(picked, 1), 1, 2)).reshape(2 * own, block)
    own_rows = lax.dynamic_slice_in_dim(symmetric, y * own, own, 0)
    positions = y * own + jnp.arange(own, dtype=jnp.int32)
    onehot = (
        (positions // block)[:, None] == jnp.arange(per_pair, dtype=jnp.int32)[None, :]
    ).astype(jnp.float32)
    terr = (onehot[:, :, None] * own_rows[:, None, :]).reshape(own, 2 * own)

    products = dot_high(jnp.concatenate([top, low], 0).astype(jnp.float32), v)
    products = products + dot_high(terr, near)

    table = np.zeros((zs, n_col, 4), np.int32)
    for col in range(n_col):
        jobs = []
        for zz in range(zs):
            ks = [(pos_of[2 * zz + yy] - pos_of[col]) % n_col for yy in range(2)]
            ready = max(min(k, n_col - k) for k in ks)
            jobs.append((ready, zz, ks))
        for j, (_, zz, ks) in enumerate(sorted(jobs)):
            table[j, col] = [zz, ks[0], ks[1], int(zz == col // 2)]
    row_spots = jnp.bitwise_xor(r, jnp.arange(n_row, dtype=jnp.int32))
    out = jax.ShapeDtypeStruct((n_row * own, n_col * own), jnp.float32)
    for j in range(zs):
        cands = tuple(sorted(set(table[j, :, 1:3].ravel().tolist())))
        scalars = jnp.concatenate([jnp.asarray(table[j])[c], row_spots])
        out = tile_job(scalars, cands, bufs, rows, terr, out)
    return out.reshape(n_row, 1, own, n_col * own), products


def power_of_two(n):
    return n > 1 and n & (n - 1) == 0


def solution(mesh):
    n_row, n_col = mesh.shape["row"], mesh.shape["col"]

    def body(design, arc_filter, arc_of_row, terr_stored, block_order, directions):
        args = (design, arc_filter, arc_of_row, terr_stored, block_order, directions)
        own, block = design.shape[0], terr_stored.shape[1]
        aligned = own % 32 == 0 and (2 * own) % block == 0 and (2 * own) % 128 == 0
        if power_of_two(n_row) and power_of_two(n_col) and n_col > 6 and aligned:
            return ring_body(n_row, n_col, *args)
        return general_body(*args)

    return jax.shard_map(
        body,
        mesh=mesh,
        in_specs=(
            P(("row", "col"), None),
            P(),
            P(),
            P(("row", "col"), None),
            P("row"),
            P(("row", "col"), None),
        ),
        out_specs=(P(None, "col", None, "row"), P(("row", "col"), None)),
        check_vma=False,
    )
```
